32 devices in a mesh: dp: 4 (over y, x), fsdp: 8 (over z, core).
Axes of the slice: x: 2, y: 2, z: 4, core: 2. Of those that a mesh axis runs over, the one named last changes fastest.
Arguments:
- activations: bfloat16 [4096, 4096], P('fsdp'), may hold values from -6 to 6
- cotangent: bfloat16 [4096, 14336], P('fsdp', 'dp'), may hold values from -6 to 6
- next_input: bfloat16 [4096, 4096], P('fsdp'), may hold values from -6 to 6
- next_weight: bfloat16 [4096, 14336], P('fsdp', 'dp'), may hold values from -0.09375 to 0.09375
- master: float32 [4096, 14336], P('fsdp', 'dp'), may hold values from -0.0625 to 0.0625
- first_moment: float32 [4096, 14336], P('fsdp', 'dp'), may hold values from -0.12 to 0.12
- second_moment: float32 [4096, 14336], P('fsdp', 'dp'), may hold values from 1e-05 to 0.0003
- token_counts: int32 [8], P('fsdp'), may hold values from 128 to 512, as said below
- peer_groups: int32 [4], replicated, may hold values from 0 to 3, as said below
Outputs:
- next_output: bfloat16 [4096, 14336], P('fsdp', 'dp')
- new_master: float32 [4096, 14336], P('fsdp', 'dp')
- new_first: float32 [4096, 14336], P('fsdp', 'dp')
- new_second: float32 [4096, 14336], P('fsdp', 'dp')
- copy_master: float32 [4096, 14336], P('fsdp', 'dp')
- copy_first: float32 [4096, 14336], P('fsdp', 'dp')
- copy_second: float32 [4096, 14336], P('fsdp', 'dp')
The draws below stay inside these ranges and needn't reach their ends.
Inputs may be any that keep to these rules, and one draw needn't show every extreme that they name: token_counts[k] is the number of live rows in block k of 512 rows; rows at or past it are padding. peer_groups[g] = (g + s) mod 4 for one s from 1 to 3, the same s for every g.
All inputs are finite; a program needn't handle non-finite values.
Results may differ from the reference program's by a relative error of at most 0.025.
Values may be sent and summed in bfloat16 or wider, within the bound.
A program may use at most 192 MiB of HBM per device.

```python
import math
import jax
import jax.numpy as jnp
from jax import lax

D = 8192
MODEL_WIN = 4096
HIDDEN_WIN = 14336
TOK_DEV = 512
TOKENS = 4096
N_DP = 4
N_FSDP = 8


def draw_token_counts(key, part):
    indices = jnp.arange(N_FSDP, dtype=jnp.int32)
    lowest = TOK_DEV // 4
    rising = lowest + (TOK_DEV - lowest) * indices // max(N_FSDP - 1, 1)
    jitter = jax.random.randint(jax.random.fold_in(key, 11), (N_FSDP,), 0, TOK_DEV // 8 + 1)
    counts = jnp.maximum(rising - jitter, lowest)
    return counts.at[N_FSDP - 1].set(TOK_DEV).astype(jnp.int32)


def draw_peer_groups(key, part):
    mixed = jax.random.fold_in(jax.random.fold_in(key, 29), 1)
    raw_value = jax.random.randint(mixed, (), 0, 1048576)
    shift_by = 1 + raw_value % (N_DP - 1)
    return ((jnp.arange(N_DP, dtype=jnp.int32) + shift_by) % N_DP).astype(jnp.int32)


def levels(stream_key, extent, cuts, smallest, top_value):
    gain, own = 1.0, jax.random.fold_in(stream_key, 6)
    for dim, blocks in cuts:
        heights = jnp.exp(jax.random.uniform(jax.random.fold_in(own, dim), (blocks,), jnp.float32, smallest / len(cuts), top_value / len(cuts)))
        gain = gain * jnp.repeat(heights, extent[dim] // blocks).reshape([-1 if axis == dim else 1 for axis in range(len(extent))])
    return gain


def centred(rng, dims, width, limit, pieces=(), held_as=jnp.bfloat16):
    array = width * jax.random.normal(rng, dims, jnp.float32)
    if pieces:
        array = array * levels(rng, dims, pieces, -0.22, 0.18)
    return jnp.clip(array, -limit, limit).astype(held_as)


def setup_inputs(seed: int = 0) -> dict:
    splits = jax.random.split(jax.random.key(seed), 10)
    return {
        "activations": centred(splits[0], (TOKENS, MODEL_WIN), 1.0, 6.0, ((0, 8),)),
        "cotangent": centred(splits[1], (TOKENS, HIDDEN_WIN), 1.0, 6.0, ((0, 8), (1, 4))),
        "next_input": centred(splits[2], (TOKENS, MODEL_WIN), 1.0, 6.0, ((0, 8),)),
        "next_weight": centred(splits[3], (MODEL_WIN, HIDDEN_WIN), MODEL_WIN ** -0.5, 0.09375, ((0, 8), (1, 4))),
        "master": centred(splits[4], (MODEL_WIN, HIDDEN_WIN), D ** -0.5, 0.0625, ((0, 8), (1, 4)), jnp.float32),
        "first_moment": centred(splits[5], (MODEL_WIN, HIDDEN_WIN), 0.02, 0.12, ((0, 8), (1, 4)), jnp.float32),
        "second_moment": jnp.clip(jnp.exp(math.log(0.0003) - 3.4011975 * jax.random.uniform(splits[6], (MODEL_WIN, HIDDEN_WIN), jnp.float32) ** levels(splits[6], (MODEL_WIN, HIDDEN_WIN), ((0, 8), (1, 4)), -0.2, 0.2)), 9.999999747378752e-06, 0.0003),
        "token_counts": draw_token_counts(jax.random.fold_in(splits[9], 71), 0),
        "peer_groups": draw_peer_groups(jax.random.fold_in(splits[9], 71), 0),
    }


beta_first = 0.9
beta_second = 0.95
epsilon = 1e-05
learn_rate = 0.00015
decay_rate = 0.1

def adam_update(master, first_moment, second_moment, gradient):
    new_first = beta_first * first_moment + (1.0 - beta_first) * gradient
    new_second = beta_second * second_moment + (1.0 - beta_second) * gradient * gradient
    new_master = master - learn_rate * (new_first / (jnp.sqrt(new_second) + epsilon) + decay_rate * master)
    return (new_master, new_first, new_second)

def reference(activations, cotangent, next_input, next_weight, master, first_moment, second_moment, token_counts, peer_groups):
    input_blocks = activations.reshape(N_FSDP, TOK_DEV, MODEL_WIN)
    positions = jnp.arange(TOK_DEV, dtype=jnp.int32)
    live_rows = positions[None, :] < token_counts[:, None]
    masked = jnp.where(live_rows[:, :, None], cotangent.reshape(N_FSDP, TOK_DEV, HIDDEN_WIN), jnp.zeros((), cotangent.dtype))

    def accumulate(running, operands):
        input_block, cotangent_block = operands
        product = lax.dot_general(input_block, cotangent_block, (((0,), (0,)), ((), ())), preferred_element_type=jnp.float32)
        rounded = lax.optimization_barrier(product.astype(jnp.bfloat16))
        return (running + rounded.astype(jnp.float32), None)
    grad_sum, ignored = lax.scan(accumulate, jnp.zeros((MODEL_WIN, HIDDEN_WIN), jnp.float32), (input_blocks, masked))
    token_total = jnp.sum(token_counts).astype(jnp.float32)
    gradient = grad_sum / token_total
    new_master, new_first, new_second = adam_update(master, first_moment, second_moment, gradient)
    source = jnp.zeros((N_DP,), jnp.int32).at[peer_groups].set(jnp.arange(N_DP, dtype=jnp.int32))

    def copy_of(state):
        blocks = state.reshape(MODEL_WIN, N_DP, HIDDEN_WIN // N_DP)
        return jnp.take(blocks, source, axis=1).reshape(MODEL_WIN, HIDDEN_WIN)
    next_output = jnp.dot(next_input, next_weight, preferred_element_type=jnp.float32).astype(jnp.bfloat16)
    return (next_output, new_master, new_first, new_second, copy_of(new_master), copy_of(new_first), copy_of(new_second))
```

```python
from functools import partial

import jax
import jax.numpy as jnp
from jax import lax
from jax.experimental import pallas as pl
from jax.experimental.pallas import tpu as pltpu
from jax.sharding import PartitionSpec as P

beta_first = 0.9
beta_second = 0.95
epsilon = 1e-05
learn_rate = 0.00015
decay_rate = 0.1

MESH = pl.DeviceIdType.MESH
WIDTH = 128
HOP = 2
RELAY = 2
LEAD = 6
PARTS = 8
STAGES = 8
BLOCK = 256


def adam_update(master, first_moment, second_moment, gradient):
    new_first = beta_first * first_moment + (1.0 - beta_first) * gradient
    new_second = beta_second * second_moment + (1.0 - beta_second) * gradient * gradient
    new_master = master - learn_rate * (
        new_first / (jnp.sqrt(new_second) + epsilon) + decay_rate * master
    )
    return (new_master, new_first, new_second)


def kernel(
    chips, groups, chunks, distance,
    count, inputs, cotangent, weight, master, first, second,
    gathered, out_master, out_first, out_second, copies,
    loaded, outgoing, turned, rights, counts, paired, arrived, state, fresh, staged,
    count_send, count_recv, load_sem, turn_send, turn_recv, right_send, right_recv, right_sem,
    line_send, line_recv, gather_send, gather_recv, whole_send, whole_recv,
    twin_send, twin_recv, copy_send, copy_recv, state_sem, fresh_sem, keep_sem,
):
    g = lax.axis_index("dp")
    f = lax.axis_index("fsdp")
    z = f // 2
    core = f % 2
    members = 2 * chips
    rows = weight.shape[0]
    piece = rows // PARTS
    last = chips - 1
    finish = HOP * last
    twin = (g, z * 2 + 1 - core)
    right = (g, ((z + 1) % chips) * 2 + core)
    left = (g, ((z + chips - 1) % chips) * 2 + core)
    peer = ((g + distance) % groups, f)
    giver = ((g + groups - distance) % groups, f)

    def cols(c):
        return pl.ds(pl.multiple_of(c * WIDTH, WIDTH), WIDTH)

    def remote(src, dst, send, recv, device):
        return pltpu.make_async_remote_copy(
            src_ref=src, dst_ref=dst, send_sem=send, recv_sem=recv,
            device_id=device, device_id_type=MESH,
        )

    def count_copy(k, slot, device):
        part = counts.at[slot]
        return remote(part, part, count_send.at[k], count_recv.at[k], device)

    def input_load(d, plane, slot):
        start = pl.multiple_of((2 * d + plane) * rows, rows)
        return pltpu.make_async_copy(inputs.at[:, pl.ds(start, rows)], loaded.at[slot], load_sem.at[slot])

    def turn_copy(d):
        return remote(outgoing.at[d], turned.at[1, d], turn_send.at[d], turn_recv.at[d], twin)

    def line_copy(c, d, slot, device):
        return remote(paired.at[c, d], arrived.at[c, slot],
                      line_send.at[c, d], line_recv.at[c, slot], device)

    def first_gather(c, way, device):
        return remote(weight.at[:, cols(c)], gathered.at[z, core, :, cols(c)],
                      gather_send.at[c, chips if way else z], gather_recv.at[c, z], device)

    def gather_copy(c, o, device):
        part = gathered.at[o, core, :, cols(c)]
        return remote(part, part, gather_send.at[c, o], gather_recv.at[c, o], device)

    def twin_copy(c, o):
        part = gathered.at[o, core, :, cols(c)]
        return remote(part, part, twin_send.at[c, o], twin_recv.at[c, o], twin)

    def twin_arrival(c, o):
        part = gathered.at[o, 1 - core, :, cols(c)]
        return remote(part, part, twin_send.at[c, o], twin_recv.at[c, o], twin)

    def peer_copy(c):
        return remote(staged.at[c % STAGES], copies.at[:, :, cols(c)], copy_send.at[c], copy_recv.at[c], peer)

    def state_loads(c):
        return [
            pltpu.make_async_copy(ref.at[:, cols(c)], state.at[c % 2, i], state_sem.at[c % 2, i])
            for i, ref in enumerate((master, first, second))
        ]

    def fresh_stores(c):
        return [
            pltpu.make_async_copy(fresh.at[c % 2, i], ref.at[:, cols(c)], fresh_sem.at[c % 2, i])
            for i, ref in enumerate((out_master, out_first, out_second))
        ]

    def add_into(c, d, ref):
        @pl.loop(0, PARTS)
        def _(i):
            part = pl.ds(pl.multiple_of(i * piece, piece), piece)
            total_part = paired[c, d, part, :].astype(jnp.float32) + ref[part, :].astype(jnp.float32)
            paired[c, d, part, :] = total_part.astype(jnp.bfloat16)

    def within(c):
        return jnp.logical_and(c >= 0, c < chunks)

    def issued(t, position):
        total = LEAD + (t + 1)
        for k in range(1, chips):
            total = total + jnp.where(
                position + k <= last, jnp.minimum(t + 1, HOP * (last - k)), 0
            )
            total = total + jnp.where(k <= position, jnp.minimum(t + 1, RELAY * k), 0)
        return jnp.minimum(total, chunks)

    def send_own(low_right, high_right, low_left, high_left):
        @pl.when(z < last)
        def _():
            @pl.loop(low_right, high_right)
            def _(c):
                first_gather(c, 0, right).start()

        @pl.when(z > 0)
        def _():
            @pl.loop(low_left, high_left)
            def _(c):
                first_gather(c, 1, left).start()

    barrier = pltpu.get_barrier_semaphore()
    others = [(g, (f + k) % members) for k in range(1, members)]
    greeted = others + [peer, giver]
    for device in greeted:
        pl.semaphore_signal(barrier, inc=1, device_id=device, device_id_type=MESH)
    pl.semaphore_wait(barrier, len(greeted))

    send_own(0, LEAD, 0, LEAD)
    right_copy = remote(cotangent, rights.at[1], right_send, right_recv, twin)
    right_copy.start()
    right_load = pltpu.make_async_copy(cotangent, rights.at[0], right_sem)
    right_load.start()
    order = [(d, 1) for d in range(chips)] + [(d, 0) for d in range(chips)]

    def turn_load(k):
        d, mine = order[k]
        return input_load(d, 1 - core if mine else core, k % 2)

    turn_load(0).start()
    whole_copy = remote(weight, gathered.at[z, core], whole_send, whole_recv, twin)
    whole_copy.start()
    keep = pltpu.make_async_copy(weight, gathered.at[z, core], keep_sem)
    keep.start()
    counts[f] = jnp.full(counts.shape[1:], count[0].astype(jnp.float32))
    for k, device in enumerate(others):
        count_copy(k, f, device).start()

    for k in range(2 * chips):
        if k + 1 < 2 * chips:
            turn_load(k + 1).start()
        turn_load(k).wait()
        d, mine = order[k]
        block = loaded[k % 2]
        live = lax.broadcasted_iota(jnp.int32, block.shape, 0) < count[0]
        block = jnp.where(live, block, jnp.zeros((), block.dtype)).T
        if mine:
            outgoing[d] = block
            turn_copy(d).start()
        else:
            turned[0, d] = block

    def multiply(j):
        wide = pl.ds(pl.multiple_of(j * (2 * WIDTH), 2 * WIDTH), 2 * WIDTH)

        @pl.loop(0, chips)
        def _(d):
            product = jnp.dot(turned[0, d], rights[0, :, wide], preferred_element_type=jnp.float32)
            product += jnp.dot(turned[1, d], rights[1, :, wide], preferred_element_type=jnp.float32)
            product = product.astype(jnp.bfloat16)
            paired[2 * j, d] = product[:, :WIDTH]
            paired[2 * j + 1, d] = product[:, WIDTH:]

    right_load.wait()
    right_copy.wait_recv()
    for d in range(chips):
        turn_copy(d).wait_recv()
    multiply(0)
    for k in range(members - 1):
        count_copy(k, (f + members - 1 - k) % members, others[k]).wait_recv()

    def update(c, refs):
        slot = c % 2
        share = 1.0 / jnp.sum(counts[:, :1, :], axis=0)

        @pl.loop(0, PARTS)
        def _(i):
            part = pl.ds(pl.multiple_of(i * piece, piece), piece)
            gradient = paired[c, z, part, :].astype(jnp.float32)
            for ref in refs:
                gradient += ref[part, :].astype(jnp.float32)
            results = adam_update(
                state[slot, 0, part, :], state[slot, 1, part, :], state[slot, 2, part, :], gradient * share
            )
            for k, value in enumerate(results):
                fresh[slot, k, part, :] = value
                staged[c % STAGES, k, part, :] = value.astype(jnp.bfloat16)

    @pl.loop(0, chunks + finish)
    def _(t):
        coming = t + 1 - finish

        @pl.when(within(coming))
        def _():
            for copy in state_loads(coming):
                copy.start()

        for d in range(chips):
            e = last - d
            rightward = t - HOP * (z + last - e)

            @pl.when(jnp.logical_and(z < e, within(rightward)))
            def _():
                @pl.when(z > 0)
                def _():
                    line_copy(rightward, e, e, left).wait_recv()
                    add_into(rightward, e, arrived.at[rightward, e])

                line_copy(rightward, e, e, right).start()

            leftward = t - HOP * (last - z + d)

            @pl.when(jnp.logical_and(z > d, within(leftward)))
            def _():
                @pl.when(z < last)
                def _():
                    line_copy(leftward, d, d, right).wait_recv()
                    add_into(leftward, d, arrived.at[leftward, d])

                @pl.when(z == d + 1)
                def _():
                    line_copy(leftward, d, chips, left).start()

                @pl.when(z > d + 1)
                def _():
                    line_copy(leftward, d, d, left).start()

        send_own(issued(t - 1, z), issued(t, z), issued(t - 1, last - z), issued(t, last - z))

        for o in range(chips):
            from_left = t - RELAY * (z - o)
            from_right = t - RELAY * (o - z)

            @pl.when(jnp.logical_and(z > o, within(from_left)))
            def _():
                gather_copy(from_left, o, left).wait_recv()

                @pl.when(z < last)
                def _():
                    gather_copy(from_left, o, right).start()

                twin_copy(from_left, o).start()

            @pl.when(jnp.logical_and(z < o, within(from_right)))
            def _():
                gather_copy(from_right, o, right).wait_recv()

                @pl.when(z > 0)
                def _():
                    gather_copy(from_right, o, left).start()

                twin_copy(from_right, o).start()

        done = t - finish

        @pl.when(within(done))
        def _():
            for copy in state_loads(done):
                copy.wait()

            @pl.when(done >= 2)
            def _():
                for copy in fresh_stores(done - 2):
                    copy.wait()

            @pl.when(done >= STAGES)
            def _():
                peer_copy(done - STAGES).wait_send()

            @pl.when(z > 0)
            def _():
                for d in range(1, chips):
                    @pl.when(z == d)
                    def _():
                        line_copy(done, d, d, left).wait_recv()

            @pl.when(z < last)
            def _():
                line_copy(done, 0, chips, right).wait_recv()

            @pl.when(z == 0)
            def _():
                update(done, [arrived.at[done, chips]])

            @pl.when(z == last)
            def _():
                update(done, [arrived.at[done, last]])

            @pl.when(jnp.logical_and(z > 0, z < last))
            def _():
                update(done, [arrived.at[done, z], arrived.at[done, chips]])

            peer_copy(done).start()
            for copy in fresh_stores(done):
                copy.start()

        @pl.when(jnp.logical_and(t % 2 == 1, t + 1 < chunks))
        def _():
            multiply((t + 1) // 2)

    keep.wait()
    right_copy.wait_send()
    whole_copy.wait()
    for d in range(chips):
        turn_copy(d).wait_send()
    for k in range(members - 1):
        count_copy(k, f, others[k]).wait_send()
    for c in range(max(chunks - 2, 0), chunks):
        for copy in fresh_stores(c):
            copy.wait()
    for c in range(max(chunks - STAGES, 0), chunks):
        peer_copy(c).wait_send()

    @pl.loop(0, chunks)
    def _(c):
        peer_copy(c).wait_recv()

        @pl.when(z < last)
        def _():
            first_gather(c, 0, right).wait_send()

        @pl.when(z > 0)
        def _():
            first_gather(c, 1, left).wait_send()

        for o in range(chips):
            @pl.when(z != o)
            def _():
                twin_arrival(c, o).wait_recv()
                twin_copy(c, o).wait_send()
                line_copy(c, o, o, right).wait_send()

            @pl.when(jnp.logical_and(z > o, z < last))
            def _():
                gather_copy(c, o, right).wait_send()

            @pl.when(jnp.logical_and(z < o, z > 0))
            def _():
                gather_copy(c, o, left).wait_send()


def exchange(distance, count, inputs, cotangent, weight, master, first, second):
    groups, members = lax.axis_size("dp"), lax.axis_size("fsdp")
    rows, columns = weight.shape
    tokens = inputs.shape[0]
    chips, chunks = members // 2, columns // WIDTH
    whole = pl.BlockSpec(memory_space=pl.ANY)
    dma = pltpu.SemaphoreType.DMA
    block = (rows, WIDTH)
    return pl.pallas_call(
        partial(kernel, chips, groups, chunks, distance),
        out_shape=(
            jax.ShapeDtypeStruct((chips, 2, rows, columns), weight.dtype),
            jax.ShapeDtypeStruct(master.shape, master.dtype),
            jax.ShapeDtypeStruct(first.shape, first.dtype),
            jax.ShapeDtypeStruct(second.shape, second.dtype),
            jax.ShapeDtypeStruct((3, rows, columns), jnp.bfloat16),
        ),
        in_specs=[pl.BlockSpec(memory_space=pltpu.SMEM)] + [whole] * 6,
        out_specs=(whole,) * 5,
        scratch_shapes=[
            pltpu.VMEM((2, tokens, rows), jnp.bfloat16),
            pltpu.VMEM((chips, rows, tokens), jnp.bfloat16),
            pltpu.VMEM((2, chips, rows, tokens), jnp.bfloat16),
            pltpu.VMEM((2, tokens, columns), jnp.bfloat16),
            pltpu.VMEM((members, 8, 128), jnp.float32),
            pltpu.VMEM((chunks, chips) + block, jnp.bfloat16),
            pltpu.VMEM((chunks, chips + 1) + block, jnp.bfloat16),
            pltpu.VMEM((2, 3) + block, jnp.float32),
            pltpu.VMEM((2, 3) + block, jnp.float32),
            pltpu.VMEM((STAGES, 3) + block, jnp.bfloat16),
            dma((members,)), dma((members,)),
            dma((2,)), dma((chips,)), dma((chips,)), dma(()), dma(()), dma(()),
            dma((chunks, chips)), dma((chunks, chips + 1)),
            dma((chunks, chips + 1)), dma((chunks, chips)),
            dma(()), dma(()),
            dma((chunks, chips)), dma((chunks, chips)),
            dma((chunks,)), dma((chunks,)),
            dma((2, 3)), dma((2, 3)), dma(()),
        ],
        compiler_params=pltpu.CompilerParams(
            collective_id=distance, has_side_effects=True, vmem_limit_bytes=60 * 1024 * 1024
        ),
        name=f"exchange_{distance}",
    )(count, inputs, cotangent, weight, master, first, second)


def finish_kernel(tokens, weights, states, copies, forward, *outs):
    forward[...] = jnp.dot(
        tokens[...], weights[...], preferred_element_type=jnp.float32
    ).astype(forward.dtype)
    for i in range(3):
        outs[i][...] = states[i][...]
        outs[3 + i][...] = copies[i].astype(jnp.float32)


def finish(tokens, gathered, states, copies):
    count, features = tokens.shape
    rows, columns = states[0].shape
    tile = pl.BlockSpec((rows, BLOCK), lambda j: (0, j))

    def body(tokens, weights, a, b, c, copies, *outs):
        finish_kernel(tokens, weights, (a, b, c), copies, *outs)

    return pl.pallas_call(
        body,
        grid=(columns // BLOCK,),
        in_specs=[
            pl.BlockSpec((count, features), lambda j: (0, 0)),
            pl.BlockSpec((features, BLOCK), lambda j: (0, j)),
            tile, tile, tile,
            pl.BlockSpec((3, rows, BLOCK), lambda j: (0, 0, j)),
        ],
        out_specs=[pl.BlockSpec((count, BLOCK), lambda j: (0, j))] + [tile] * 6,
        out_shape=[jax.ShapeDtypeStruct((count, columns), jnp.bfloat16)]
        + [jax.ShapeDtypeStruct((rows, columns), jnp.float32)] * 6,
        compiler_params=pltpu.CompilerParams(vmem_limit_bytes=56 * 1024 * 1024),
        name="finish",
    )(tokens, gathered, *states, copies)


def body(
    activations,
    cotangent,
    next_input,
    next_weight,
    master,
    first_moment,
    second_moment,
    token_counts,
    peer_groups,
):
    groups, members = lax.axis_size("dp"), lax.axis_size("fsdp")
    rows, columns = next_weight.shape
    branches = [partial(exchange, distance) for distance in range(1, groups)]
    gathered, *states, copies = lax.switch(
        jnp.clip(peer_groups[0] - 1, 0, groups - 2), branches,
        token_counts, activations, cotangent, next_weight, master, first_moment, second_moment,
    )
    return tuple(finish(next_input, gathered.reshape(members * rows, columns), states, copies))


def solution(mesh):
    return jax.shard_map(
        body,
        mesh=mesh,
        in_specs=(
            P("fsdp", None),
            P("fsdp", "dp"),
            P("fsdp", None),
            P("fsdp", "dp"),
            P("fsdp", "dp"),
            P("fsdp", "dp"),
            P("fsdp", "dp"),
            P("fsdp"),
            P(),
        ),
        out_specs=(P("fsdp", "dp"),) * 7,
        check_vma=False,
    )
```

```python
from functools import partial

import jax
import jax.numpy as jnp
from jax import lax
from jax.experimental import pallas as pl
from jax.experimental.pallas import tpu as pltpu
from jax.sharding import PartitionSpec as P

beta_first = 0.9
beta_second = 0.95
epsilon = 1e-05
learn_rate = 0.00015
decay_rate = 0.1

MESH = pl.DeviceIdType.MESH
WIDTH = 128
HOP = 1
RELAY = 1
LEAD = 6
PARTS = 8
STAGES = 8
BAND = 32


def adam_update(master, first_moment, second_moment, gradient):
    new_first = beta_first * first_moment + (1.0 - beta_first) * gradient
    new_second = beta_second * second_moment + (1.0 - beta_second) * gradient * gradient
    new_master = master - learn_rate * (
        new_first / (jnp.sqrt(new_second) + epsilon) + decay_rate * master
    )
    return (new_master, new_first, new_second)


def kernel(
    chips, groups, chunks, distance,
    count, inputs, cotangent, tokens, weight, master, first, second,
    gathered, forward, out_master, out_first, out_second, copies,
    loaded, outgoing, turned, rights, counts, paired, arrived, state, fresh, staged,
    held, summed, result,
    count_send, count_recv, load_sem, turn_send, turn_recv, right_send, right_recv, right_sem,
    line_send, line_recv, gather_send, gather_recv, whole_send, whole_recv,
    twin_send, twin_recv, copy_send, copy_recv, state_sem, fresh_sem, held_sem, wide_sem, result_sem,
):
    g = lax.axis_index("dp")
    f = lax.axis_index("fsdp")
    z = f // 2
    core = f % 2
    members = 2 * chips
    rows = weight.shape[0]
    piece = rows // PARTS
    last = chips - 1
    finish = HOP * last
    twin = (g, z * 2 + 1 - core)
    right = (g, ((z + 1) % chips) * 2 + core)
    left = (g, ((z + chips - 1) % chips) * 2 + core)
    peer = ((g + distance) % groups, f)
    giver = ((g + groups - distance) % groups, f)

    def cols(c):
        return pl.ds(pl.multiple_of(c * WIDTH, WIDTH), WIDTH)

    def remote(src, dst, send, recv, device):
        return pltpu.make_async_remote_copy(
            src_ref=src, dst_ref=dst, send_sem=send, recv_sem=recv,
            device_id=device, device_id_type=MESH,
        )

    def count_copy(k, slot, device):
        part = counts.at[slot]
        return remote(part, part, count_send.at[k], count_recv.at[k], device)

    def input_load(d, plane, slot):
        start = pl.multiple_of((2 * d + plane) * rows, rows)
        return pltpu.make_async_copy(inputs.at[:, pl.ds(start, rows)], loaded.at[slot], load_sem.at[slot])

    def turn_copy(d):
        return remote(outgoing.at[d], turned.at[1, d], turn_send.at[d], turn_recv.at[d], twin)

    def line_copy(c, d, slot, device):
        return remote(paired.at[c, d], arrived.at[c, slot],
                      line_send.at[c, d], line_recv.at[c, slot], device)

    def first_gather(c, way, device):
        return remote(weight.at[:, cols(c)], gathered.at[z, core, :, cols(c)],
                      gather_send.at[c, chips if way else z], gather_recv.at[c, z], device)

    def gather_copy(c, o, device):
        part = gathered.at[o, core, :, cols(c)]
        return remote(part, part, gather_send.at[c, o], gather_recv.at[c, o], device)

    def twin_copy(c, o):
        part = gathered.at[o, core, :, cols(c)]
        return remote(part, part, twin_send.at[c, o], twin_recv.at[c, o], twin)

    def twin_arrival(c, o):
        part = gathered.at[o, 1 - core, :, cols(c)]
        return remote(part, part, twin_send.at[c, o], twin_recv.at[c, o], twin)

    def peer_copy(c):
        return remote(staged.at[c % STAGES], copies.at[:, :, cols(c)], copy_send.at[c], copy_recv.at[c], peer)

    def state_loads(c):
        return [
            pltpu.make_async_copy(ref.at[:, cols(c)], state.at[c % 2, i], state_sem.at[c % 2, i])
            for i, ref in enumerate((master, first, second))
        ]

    def fresh_stores(c):
        return [
            pltpu.make_async_copy(fresh.at[c % 2, i], ref.at[:, cols(c)], fresh_sem.at[c % 2, i])
            for i, ref in enumerate((out_master, out_first, out_second))
        ]

    def wide(j):
        return pl.ds(pl.multiple_of(j * (2 * WIDTH), 2 * WIDTH), 2 * WIDTH)

    def wide_load(j, o, q, source):
        return pltpu.make_async_copy(
            source, outgoing.at[o, :, pl.ds(q * 2 * WIDTH, 2 * WIDTH)], wide_sem.at[o, q],
        )

    def start_wide(j):
        for o in range(chips):
            wide_load(j, o, 1, gathered.at[o, 1 - core, :, wide(j)]).start()

            @pl.when(z == o)
            def _():
                wide_load(j, o, 0, weight.at[:, wide(j)]).start()

            @pl.when(z != o)
            def _():
                wide_load(j, o, 0, gathered.at[o, core, :, wide(j)]).start()

    def wait_wide(j):
        for o in range(chips):
            for q in range(2):
                wide_load(j, o, q, weight.at[:, wide(j)]).wait()

    def result_store(j):
        return pltpu.make_async_copy(result.at[j % 2], forward.at[:, wide(j)], result_sem.at[j % 2])

    def add_into(c, d, ref):
        @pl.loop(0, PARTS)
        def _(i):
            part = pl.ds(pl.multiple_of(i * piece, piece), piece)
            total_part = paired[c, d, part, :].astype(jnp.float32) + ref[part, :].astype(jnp.float32)
            paired[c, d, part, :] = total_part.astype(jnp.bfloat16)

    def within(c):
        return jnp.logical_and(c >= 0, c < chunks)

    def issued(t, position):
        total = LEAD + (t + 1)
        for k in range(1, chips):
            total = total + jnp.where(
                position + k <= last, jnp.minimum(t + 1, HOP * (last - k)), 0
            )
            total = total + jnp.where(k <= position, jnp.minimum(t + 1, RELAY * k), 0)
        return jnp.minimum(total, chunks)

    def send_own(low_right, high_right, low_left, high_left):
        @pl.when(z < last)
        def _():
            @pl.loop(low_right, high_right)
            def _(c):
                first_gather(c, 0, right).start()

        @pl.when(z > 0)
        def _():
            @pl.loop(low_left, high_left)
            def _(c):
                first_gather(c, 1, left).start()

    barrier = pltpu.get_barrier_semaphore()
    others = [(g, (f + k) % members) for k in range(1, members)]
    greeted = others + [peer, giver]
    for device in greeted:
        pl.semaphore_signal(barrier, inc=1, device_id=device, device_id_type=MESH)
    pl.semaphore_wait(barrier, len(greeted))

    send_own(0, LEAD, 0, LEAD)
    right_copy = remote(cotangent, rights.at[1], right_send, right_recv, twin)
    right_copy.start()
    right_load = pltpu.make_async_copy(cotangent, rights.at[0], right_sem)
    right_load.start()
    order = [(d, 1) for d in range(chips)] + [(d, 0) for d in range(chips)]

    def turn_load(k):
        d, mine = order[k]
        return input_load(d, 1 - core if mine else core, k % 2)

    turn_load(0).start()
    whole_copy = remote(weight, gathered.at[z, core], whole_send, whole_recv, twin)
    whole_copy.start()
    held_load = pltpu.make_async_copy(tokens, held, held_sem)
    held_load.start()
    counts[f] = jnp.full(counts.shape[1:], count[0].astype(jnp.float32))
    for k, device in enumerate(others):
        count_copy(k, f, device).start()

    for k in range(2 * chips):
        if k + 1 < 2 * chips:
            turn_load(k + 1).start()
        turn_load(k).wait()
        d, mine = order[k]
        block = loaded[k % 2]
        live = lax.broadcasted_iota(jnp.int32, block.shape, 0) < count[0]
        block = jnp.where(live, block, jnp.zeros((), block.dtype)).T
        if mine:
            outgoing[d] = block
            turn_copy(d).start()
        else:
            turned[0, d] = block

    def multiply(j):
        @pl.loop(0, chips)
        def _(d):
            product = jnp.dot(turned[0, d], rights[0, :, wide(j)], preferred_element_type=jnp.float32)
            product += jnp.dot(turned[1, d], rights[1, :, wide(j)], preferred_element_type=jnp.float32)
            product = product.astype(jnp.bfloat16)
            paired[2 * j, d] = product[:, :WIDTH]
            paired[2 * j + 1, d] = product[:, WIDTH:]

    def project(j):
        wait_wide(j)

        def part(o):
            total = None
            for q, plane in enumerate((core, 1 - core)):
                start = pl.multiple_of((2 * o + plane) * rows, rows)
                product = jnp.dot(
                    held[:, pl.ds(start, rows)], outgoing[o, :, q * 2 * WIDTH:(q + 1) * 2 * WIDTH],
                    preferred_element_type=jnp.float32,
                )
                total = product if q == 0 else total + product
            return total

        summed[...] = part(0)

        @pl.loop(1, chips)
        def _(o):
            summed[...] += part(o)

        @pl.when(j >= 2)
        def _():
            result_store(j - 2).wait()

        result[j % 2] = summed[...].astype(jnp.bfloat16)
        result_store(j).start()

    right_load.wait()
    right_copy.wait_recv()
    for d in range(chips):
        turn_copy(d).wait_recv()
    multiply(0)
    for k in range(members - 1):
        count_copy(k, (f + members - 1 - k) % members, others[k]).wait_recv()

    held_load.wait()
    whole_copy.wait_recv()
    for d in range(chips):
        turn_copy(d).wait_send()

    def update(c, refs):
        slot = c % 2
        share = 1.0 / jnp.sum(counts[:, :1, :], axis=0)

        @pl.loop(0, PARTS)
        def _(i):
            part = pl.ds(pl.multiple_of(i * piece, piece), piece)
            gradient = paired[c, z, part, :].astype(jnp.float32)
            for ref in refs:
                gradient += ref[part, :].astype(jnp.float32)
            results = adam_update(
                state[slot, 0, part, :], state[slot, 1, part, :], state[slot, 2, part, :], gradient * share
            )
            for k, value in enumerate(results):
                fresh[slot, k, part, :] = value
                staged[c % STAGES, k, part, :] = value.astype(jnp.bfloat16)

    @pl.loop(0, chunks + max(finish, RELAY * last + 2))
    def _(t):
        coming = t + 1 - finish

        @pl.when(within(coming))
        def _():
            for copy in state_loads(coming):
                copy.start()

        for d in range(chips):
            e = last - d
            rightward = t - HOP * (z + last - e)

            @pl.when(jnp.logical_and(z < e, within(rightward)))
            def _():
                @pl.when(z > 0)
                def _():
                    line_copy(rightward, e, e, left).wait_recv()
                    add_into(rightward, e, arrived.at[rightward, e])

                line_copy(rightward, e, e, right).start()

            leftward = t - HOP * (last - z + d)

            @pl.when(jnp.logical_and(z > d, within(leftward)))
            def _():
                @pl.when(z < last)
                def _():
                    line_copy(leftward, d, d, right).wait_recv()
                    add_into(leftward, d, arrived.at[leftward, d])

                @pl.when(z == d + 1)
                def _():
                    line_copy(leftward, d, chips, left).start()

                @pl.when(z > d + 1)
                def _():
                    line_copy(leftward, d, d, left).start()

        send_own(issued(t - 1, z), issued(t, z), issued(t - 1, last - z), issued(t, last - z))

        for o in range(chips):
            from_left = t - RELAY * (z - o)
            from_right = t - RELAY * (o - z)

            @pl.when(jnp.logical_and(z > o, within(from_left)))
            def _():
                gather_copy(from_left, o, left).wait_recv()

                @pl.when(z < last)
                def _():
                    gather_copy(from_left, o, right).start()

                twin_copy(from_left, o).start()

            @pl.when(jnp.logical_and(z < o, within(from_right)))
            def _():
                gather_copy(from_right, o, right).wait_recv()

                @pl.when(z > 0)
                def _():
                    gather_copy(from_right, o, left).start()

                twin_copy(from_right, o).start()

        done = t - finish

        @pl.when(within(done))
        def _():
            for copy in state_loads(done):
                copy.wait()

            @pl.when(done >= 2)
            def _():
                for copy in fresh_stores(done - 2):
                    copy.wait()

            @pl.when(done >= STAGES)
            def _():
                peer_copy(done - STAGES).wait_send()

            @pl.when(z > 0)
            def _():
                for d in range(1, chips):
                    @pl.when(z == d)
                    def _():
                        line_copy(done, d, d, left).wait_recv()

            @pl.when(z < last)
            def _():
                line_copy(done, 0, chips, right).wait_recv()

            @pl.when(z == 0)
            def _():
                update(done, [arrived.at[done, chips]])

            @pl.when(z == last)
            def _():
                update(done, [arrived.at[done, last]])

            @pl.when(jnp.logical_and(z > 0, z < last))
            def _():
                update(done, [arrived.at[done, z], arrived.at[done, chips]])

            peer_copy(done).start()
            for copy in fresh_stores(done):
                copy.start()

        ready = t - RELAY * last - 1

        @pl.when(within(ready))
        def _():
            for o in range(chips):
                @pl.when(z != o)
                def _():
                    twin_arrival(ready, o).wait_recv()

            @pl.when(ready % 2 == 1)
            def _():
                start_wide(ready // 2)

        @pl.when(jnp.logical_and(within(ready - 1), ready % 2 == 0))
        def _():
            project((ready - 1) // 2)

        @pl.when(jnp.logical_and(t % 2 == 1, t + 1 < chunks))
        def _():
            multiply((t + 1) // 2)

    right_copy.wait_send()
    whole_copy.wait_send()
    for j in range(max(chunks // 2 - 2, 0), chunks // 2):
        result_store(j).wait()
    for k in range(members - 1):
        count_copy(k, f, others[k]).wait_send()
    for c in range(max(chunks - 2, 0), chunks):
        for copy in fresh_stores(c):
            copy.wait()
    for c in range(max(chunks - STAGES, 0), chunks):
        peer_copy(c).wait_send()

    @pl.loop(0, chunks)
    def _(c):
        peer_copy(c).wait_recv()

        @pl.when(z < last)
        def _():
            first_gather(c, 0, right).wait_send()

        @pl.when(z > 0)
        def _():
            first_gather(c, 1, left).wait_send()

        for o in range(chips):
            @pl.when(z != o)
            def _():
                twin_copy(c, o).wait_send()
                line_copy(c, o, o, right).wait_send()

            @pl.when(jnp.logical_and(z > o, z < last))
            def _():
                gather_copy(c, o, right).wait_send()

            @pl.when(jnp.logical_and(z < o, z > 0))
            def _():
                gather_copy(c, o, left).wait_send()


def exchange(distance, count, inputs, cotangent, tokens, weight, master, first, second):
    groups, members = lax.axis_size("dp"), lax.axis_size("fsdp")
    rows, columns = weight.shape
    span = inputs.shape[0]
    chips, chunks = members // 2, columns // WIDTH
    whole = pl.BlockSpec(memory_space=pl.ANY)
    dma = pltpu.SemaphoreType.DMA
    block = (rows, WIDTH)
    return pl.pallas_call(
        partial(kernel, chips, groups, chunks, distance),
        out_shape=(
            jax.ShapeDtypeStruct((chips, 2, rows, columns), weight.dtype),
            jax.ShapeDtypeStruct((tokens.shape[0], columns), jnp.bfloat16),
            jax.ShapeDtypeStruct(master.shape, master.dtype),
            jax.ShapeDtypeStruct(first.shape, first.dtype),
            jax.ShapeDtypeStruct(second.shape, second.dtype),
            jax.ShapeDtypeStruct((3, rows, columns), jnp.bfloat16),
        ),
        in_specs=[pl.BlockSpec(memory_space=pltpu.SMEM)] + [whole] * 7,
        out_specs=(whole,) * 6,
        scratch_shapes=[
            pltpu.VMEM((2, span, rows), jnp.bfloat16),
            pltpu.VMEM((chips, rows, span), jnp.bfloat16),
            pltpu.VMEM((2, chips, rows, span), jnp.bfloat16),
            pltpu.VMEM((2, span, columns), jnp.bfloat16),
            pltpu.VMEM((members, 8, 128), jnp.float32),
            pltpu.VMEM((chunks, chips) + block, jnp.bfloat16),
            pltpu.VMEM((chunks, chips + 1) + block, jnp.bfloat16),
            pltpu.VMEM((2, 3) + block, jnp.float32),
            pltpu.VMEM((2, 3) + block, jnp.float32),
            pltpu.VMEM((STAGES, 3) + block, jnp.bfloat16),
            pltpu.VMEM(tokens.shape, jnp.bfloat16),
            pltpu.VMEM((tokens.shape[0], 2 * WIDTH), jnp.float32),
            pltpu.VMEM((2, tokens.shape[0], 2 * WIDTH), jnp.bfloat16),
            dma((members,)), dma((members,)),
            dma((2,)), dma((chips,)), dma((chips,)), dma(()), dma(()), dma(()),
            dma((chunks, chips)), dma((chunks, chips + 1)),
            dma((chunks, chips + 1)), dma((chunks, chips)),
            dma(()), dma(()),
            dma((chunks, chips)), dma((chunks, chips)),
            dma((chunks,)), dma((chunks,)),
            dma((2, 3)), dma((2, 3)),
            dma(()), dma((chips, 2)), dma((2,)),
        ],
        compiler_params=pltpu.CompilerParams(
            collective_id=distance, has_side_effects=True, vmem_limit_bytes=63 * 1024 * 1024
        ),
        name=f"exchange_{distance}",
    )(count, inputs, cotangent, tokens, weight, master, first, second)


def finish_kernel(forward, master, first, second, copies, *outs):
    for ref, out in zip((forward, master, first, second), outs):
        out[...] = ref[...]
    for i in range(3):
        outs[4 + i][...] = copies[i].astype(jnp.float32)


def finish(forward, states, copies):
    count, columns = forward.shape
    rows = states[0].shape[0]
    steps = rows // BAND
    tile = pl.BlockSpec((BAND, columns), lambda j: (j, 0))
    front = pl.BlockSpec((count // steps, columns), lambda j: (j, 0))
    return pl.pallas_call(
        finish_kernel,
        grid=(steps,),
        in_specs=[front, tile, tile, tile, pl.BlockSpec((3, BAND, columns), lambda j: (0, j, 0))],
        out_specs=[front] + [tile] * 6,
        out_shape=[jax.ShapeDtypeStruct((count, columns), jnp.bfloat16)]
        + [jax.ShapeDtypeStruct((rows, columns), jnp.float32)] * 6,
        compiler_params=pltpu.CompilerParams(vmem_limit_bytes=56 * 1024 * 1024),
        name="finish",
    )(forward, *states, copies)


def body(
    activations,
    cotangent,
    next_input,
    next_weight,
    master,
    first_moment,
    second_moment,
    token_counts,
    peer_groups,
):
    groups = lax.axis_size("dp")
    branches = [partial(exchange, distance) for distance in range(1, groups)]
    gathered, forward, *states, copies = lax.switch(
        jnp.clip(peer_groups[0] - 1, 0, groups - 2), branches,
        token_counts, activations, cotangent, next_input, next_weight, master, first_moment, second_moment,
    )
    return tuple(finish(forward, states, copies))


def solution(mesh):
    return jax.shard_map(
        body,
        mesh=mesh,
        in_specs=(
            P("fsdp", None),
            P("fsdp", "dp"),
            P("fsdp", None),
            P("fsdp", "dp"),
            P("fsdp", "dp"),
            P("fsdp", "dp"),
            P("fsdp", "dp"),
            P("fsdp"),
            P(),
        ),
        out_specs=(P("fsdp", "dp"),) * 7,
        check_vma=False,
    )
```

```python
from functools import partial

import jax
import jax.numpy as jnp
from jax import lax
from jax.experimental import pallas as pl
from jax.experimental.pallas import tpu as pltpu
from jax.sharding import PartitionSpec as P

beta_first = 0.9
beta_second = 0.95
epsilon = 1e-05
learn_rate = 0.00015
decay_rate = 0.1

MESH = pl.DeviceIdType.MESH
WIDTH = 128
HOP = 1
RELAY = 1
AHEAD = 0
LEAD = 6
SPLIT = 1
PARTS = 8
STAGES = 8
BAND = 64


def adam_update(master, first_moment, second_moment, gradient):
    new_first = beta_first * first_moment + (1.0 - beta_first) * gradient
    new_second = beta_second * second_moment + (1.0 - beta_second) * gradient * gradient
    new_master = master - learn_rate * (
        new_first / (jnp.sqrt(new_second) + epsilon) + decay_rate * master
    )
    return (new_master, new_first, new_second)


def kernel(
    chips, groups, chunks, distance,
    count, inputs, cotangent, tokens, weight, master, first, second,
    gathered, forward, kept, copies,
    loaded, outgoing, turned, rights, counts, paired, arrived, state, staged,
    held, summed, result,
    count_send, count_recv, load_sem, turn_send, turn_recv, right_send, right_recv, right_sem,
    line_send, line_recv, gather_send, gather_recv, whole_send, whole_recv,
    twin_send, twin_recv, copy_send, copy_recv, state_sem, own_sem, held_sem, wide_sem, result_sem,
):
    g = lax.axis_index("dp")
    f = lax.axis_index("fsdp")
    z = f // 2
    core = f % 2
    members = 2 * chips
    rows = weight.shape[0]
    strip = rows // SPLIT
    piece = strip // PARTS
    units = chunks * SPLIT
    batch = 2 * SPLIT
    last = chips - 1
    finish = HOP * last
    twin = (g, z * 2 + 1 - core)
    right = (g, ((z + 1) % chips) * 2 + core)
    left = (g, ((z + chips - 1) % chips) * 2 + core)
    peer = ((g + distance) % groups, f)
    giver = ((g + groups - distance) % groups, f)

    def span(u):
        return pl.ds(pl.multiple_of((u % SPLIT) * strip, strip), strip)

    def cols(c):
        return pl.ds(pl.multiple_of(c * WIDTH, WIDTH), WIDTH)

    def area(u):
        c = u // SPLIT
        return span(u), pl.ds(pl.multiple_of(c * WIDTH, WIDTH), WIDTH)

    def remote(src, dst, send, recv, device):
        return pltpu.make_async_remote_copy(
            src_ref=src, dst_ref=dst, send_sem=send, recv_sem=recv,
            device_id=device, device_id_type=MESH,
        )

    def count_copy(k, slot, device):
        part = counts.at[slot]
        return remote(part, part, count_send.at[k], count_recv.at[k], device)

    def input_load(d, plane, slot):
        start = pl.multiple_of((2 * d + plane) * rows, rows)
        return pltpu.make_async_copy(inputs.at[:, pl.ds(start, rows)], loaded.at[slot], load_sem.at[slot])

    def turn_copy(d):
        return remote(outgoing.at[d], turned.at[1, d], turn_send.at[d], turn_recv.at[d], twin)

    def line_copy(c, d, slot, device):
        return remote(paired.at[c // SPLIT, d, span(c)], arrived.at[c // SPLIT, slot, span(c)],
                      line_send.at[c, d], line_recv.at[c, slot], device)

    def first_gather(c, way, device):
        return remote(weight.at[:, cols(c)], gathered.at[z, core, :, cols(c)],
                      gather_send.at[c, chips if way else z], gather_recv.at[c, z], device)

    def gather_copy(c, o, device):
        part = gathered.at[o, core, :, cols(c)]
        return remote(part, part, gather_send.at[c, o], gather_recv.at[c, o], device)

    def twin_copy(c, o):
        part = gathered.at[o, core, :, cols(c)]
        return remote(part, part, twin_send.at[c, o], twin_recv.at[c, o], twin)

    def twin_arrival(c, o):
        part = gathered.at[o, 1 - core, :, cols(c)]
        return remote(part, part, twin_send.at[c, o], twin_recv.at[c, o], twin)

    def peer_copy(c):
        return remote(staged.at[c % STAGES], copies.at[(slice(None),) + area(c)], copy_send.at[c], copy_recv.at[c], peer)

    def state_loads(c):
        return [
            pltpu.make_async_copy(ref.at[area(c)], state.at[c % 2, i], state_sem.at[c % 2, i])
            for i, ref in enumerate((master, first, second))
        ]

    def own_store(c):
        return pltpu.make_async_copy(
            staged.at[c % STAGES], kept.at[(slice(None),) + area(c)], own_sem.at[c % STAGES]
        )

    def wide(j):
        return pl.ds(pl.multiple_of(j * (2 * WIDTH), 2 * WIDTH), 2 * WIDTH)

    def wide_load(j, o, q, source):
        return pltpu.make_async_copy(
            source, outgoing.at[o, :, pl.ds(q * 2 * WIDTH, 2 * WIDTH)], wide_sem.at[o, q],
        )

    def start_wide(j):
        for o in range(chips):
            wide_load(j, o, 1, gathered.at[o, 1 - core, :, wide(j)]).start()

            @pl.when(z == o)
            def _():
                wide_load(j, o, 0, weight.at[:, wide(j)]).start()

            @pl.when(z != o)
            def _():
                wide_load(j, o, 0, gathered.at[o, core, :, wide(j)]).start()

    def wait_wide(j):
        for o in range(chips):
            for q in range(2):
                wide_load(j, o, q, weight.at[:, wide(j)]).wait()

    def result_store(j):
        return pltpu.make_async_copy(result.at[j % 2], forward.at[:, wide(j)], result_sem.at[j % 2])

    def add_into(u, d):
        c, base = u // SPLIT, (u % SPLIT) * strip

        @pl.loop(0, PARTS)
        def _(i):
            part = pl.ds(pl.multiple_of(base + i * piece, piece), piece)
            total_part = paired[c, d, part, :].astype(jnp.float32) + arrived[c, d, part, :].astype(jnp.float32)
            paired[c, d, part, :] = total_part.astype(jnp.bfloat16)

    def within(u):
        return jnp.logical_and(u >= 0, u < units)

    def inside(c):
        return jnp.logical_and(c >= 0, c < chunks)

    def issued(t, position):
        total = LEAD + (t + 1)
        for k in range(1, chips):
            total = total + jnp.where(
                position + k <= last, jnp.minimum(t + 1, HOP * (last - k) // SPLIT), 0
            )
            total = total + jnp.where(k <= position, jnp.minimum(t + 1, RELAY * k), 0)
        return jnp.minimum(total, chunks)

    def send_own(low_right, high_right, low_left, high_left):
        @pl.when(z < last)
        def _():
            @pl.loop(low_right, high_right)
            def _(c):
                first_gather(c, 0, right).start()

        @pl.when(z > 0)
        def _():
            @pl.loop(low_left, high_left)
            def _(c):
                first_gather(c, 1, left).start()

    barrier = pltpu.get_barrier_semaphore()
    others = [(g, (f + k) % members) for k in range(1, members)]
    greeted = others + [peer, giver]
    for device in greeted:
        pl.semaphore_signal(barrier, inc=1, device_id=device, device_id_type=MESH)
    pl.semaphore_wait(barrier, len(greeted))

    send_own(0, issued(AHEAD - 1, z), 0, issued(AHEAD - 1, last - z))
    right_copy = remote(cotangent, rights.at[1], right_send, right_recv, twin)
    right_copy.start()
    right_load = pltpu.make_async_copy(cotangent, rights.at[0], right_sem)
    right_load.start()
    order = [(d, 1) for d in range(chips)] + [(d, 0) for d in range(chips)]

    def turn_load(k):
        d, mine = order[k]
        return input_load(d, 1 - core if mine else core, k % 2)

    turn_load(0).start()
    held_load = pltpu.make_async_copy(tokens, held, held_sem)
    held_load.start()
    counts[f] = jnp.full(counts.shape[1:], count[0].astype(jnp.float32))
    for k, device in enumerate(others):
        count_copy(k, f, device).start()

    for k in range(2 * chips):
        if k + 1 < 2 * chips:
            turn_load(k + 1).start()
        turn_load(k).wait()
        d, mine = order[k]
        block = loaded[k % 2]
        live = lax.broadcasted_iota(jnp.int32, block.shape, 0) < count[0]
        block = jnp.where(live, block, jnp.zeros((), block.dtype)).T
        if mine:
            outgoing[d] = block
            turn_copy(d).start()
        else:
            turned[0, d] = block

    whole_copy = remote(weight, gathered.at[z, core], whole_send, whole_recv, twin)
    whole_copy.start()

    def multiply(j):
        @pl.loop(0, chips)
        def _(d):
            product = jnp.dot(turned[0, d], rights[0, :, wide(j)], preferred_element_type=jnp.float32)
            product += jnp.dot(turned[1, d], rights[1, :, wide(j)], preferred_element_type=jnp.float32)
            product = product.astype(jnp.bfloat16)
            paired[2 * j, d] = product[:, :WIDTH]
            paired[2 * j + 1, d] = product[:, WIDTH:]

    def project(j):
        wait_wide(j)

        def part(o):
            total = None
            for q, plane in enumerate((core, 1 - core)):
                start = pl.multiple_of((2 * o + plane) * rows, rows)
                product = jnp.dot(
                    held[:, pl.ds(start, rows)], outgoing[o, :, q * 2 * WIDTH:(q + 1) * 2 * WIDTH],
                    preferred_element_type=jnp.float32,
                )
                total = product if q == 0 else total + product
            return total

        summed[...] = part(0)

        @pl.loop(1, chips)
        def _(o):
            summed[...] += part(o)

        @pl.when(j >= 2)
        def _():
            result_store(j - 2).wait()

        result[j % 2] = summed[...].astype(jnp.bfloat16)
        result_store(j).start()

    right_load.wait()
    right_copy.wait_recv()
    for d in range(chips):
        turn_copy(d).wait_recv()
    multiply(0)
    for k in range(members - 1):
        count_copy(k, (f + members - 1 - k) % members, others[k]).wait_recv()

    def update(u, slots):
        c, base, slot = u // SPLIT, (u % SPLIT) * strip, u % 2
        share = 1.0 / jnp.sum(counts[:, :1, :], axis=0)

        @pl.loop(0, PARTS)
        def _(i):
            here = pl.ds(pl.multiple_of(base + i * piece, piece), piece)
            part = pl.ds(pl.multiple_of(i * piece, piece), piece)
            gradient = paired[c, z, here, :].astype(jnp.float32)
            for k in slots:
                gradient += arrived[c, k, here, :].astype(jnp.float32)
            results = adam_update(
                state[slot, 0, part, :], state[slot, 1, part, :], state[slot, 2, part, :], gradient * share
            )
            for k, value in enumerate(results):
                staged[u % STAGES, k, part, :] = value.astype(jnp.bfloat16)

    @pl.loop(0, units + max(finish, SPLIT * (RELAY * last + 2 - AHEAD)))
    def _(t):
        coming = t + 1 - finish

        @pl.when(within(coming))
        def _():
            for copy in state_loads(coming):
                copy.start()

        for d in range(chips):
            e = last - d
            rightward = t - HOP * (z + last - e)

            @pl.when(jnp.logical_and(z < e, within(rightward)))
            def _():
                @pl.when(z > 0)
                def _():
                    line_copy(rightward, e, e, left).wait_recv()
                    add_into(rightward, e)

                line_copy(rightward, e, e, right).start()

            leftward = t - HOP * (last - z + d)

            @pl.when(jnp.logical_and(z > d, within(leftward)))
            def _():
                @pl.when(z < last)
                def _():
                    line_copy(leftward, d, d, right).wait_recv()
                    add_into(leftward, d)

                @pl.when(z == d + 1)
                def _():
                    line_copy(leftward, d, chips, left).start()

                @pl.when(z > d + 1)
                def _():
                    line_copy(leftward, d, d, left).start()

        q = t // SPLIT + AHEAD

        @pl.when(t % SPLIT == 0)
        def _():
            send_own(issued(q - 1, z), issued(q, z), issued(q - 1, last - z), issued(q, last - z))

            for o in range(chips):
                from_left = q - RELAY * (z - o)
                from_right = q - RELAY * (o - z)

                @pl.when(jnp.logical_and(z > o, inside(from_left)))
                def _():
                    gather_copy(from_left, o, left).wait_recv()

                    @pl.when(z < last)
                    def _():
                        gather_copy(from_left, o, right).start()

                    twin_copy(from_left, o).start()

                @pl.when(jnp.logical_and(z < o, inside(from_right)))
                def _():
                    gather_copy(from_right, o, right).wait_recv()

                    @pl.when(z > 0)
                    def _():
                        gather_copy(from_right, o, left).start()

                    twin_copy(from_right, o).start()

        done = t - finish

        @pl.when(within(done))
        def _():
            for copy in state_loads(done):
                copy.wait()

            @pl.when(done >= STAGES)
            def _():
                peer_copy(done - STAGES).wait_send()
                own_store(done - STAGES).wait()

            @pl.when(z > 0)
            def _():
                for d in range(1, chips):
                    @pl.when(z == d)
                    def _():
                        line_copy(done, d, d, left).wait_recv()

            @pl.when(z < last)
            def _():
                line_copy(done, 0, chips, right).wait_recv()

            @pl.when(z == 0)
            def _():
                update(done, [chips])

            @pl.when(z == last)
            def _():
                update(done, [last])

            @pl.when(jnp.logical_and(z > 0, z < last))
            def _():
                update(done, [z, chips])

            peer_copy(done).start()
            own_store(done).start()

        ready = q - RELAY * last - 1

        @pl.when(jnp.logical_and(ready == 0, t % SPLIT == 0))
        def _():
            held_load.wait()
            whole_copy.wait_recv()
            for d in range(chips):
                turn_copy(d).wait_send()

        @pl.when(jnp.logical_and(inside(ready), t % SPLIT == 0))
        def _():
            for o in range(chips):
                @pl.when(z != o)
                def _():
                    twin_arrival(ready, o).wait_recv()

            @pl.when(ready % 2 == 1)
            def _():
                start_wide(ready // 2)

        @pl.when(jnp.logical_and(inside(ready), jnp.logical_and(ready % 2 == 1, t % SPLIT == SPLIT - 1)))
        def _():
            project(ready // 2)

        @pl.when(jnp.logical_and(t % batch == batch - 1, t + 1 < units))
        def _():
            multiply((t + 1) // batch)

    right_copy.wait_send()
    whole_copy.wait_send()
    for j in range(max(chunks // 2 - 2, 0), chunks // 2):
        result_store(j).wait()
    for k in range(members - 1):
        count_copy(k, f, others[k]).wait_send()
    for c in range(max(units - STAGES, 0), units):
        peer_copy(c).wait_send()
        own_store(c).wait()

    @pl.loop(0, units)
    def _(u):
        peer_copy(u).wait_recv()
        for o in range(chips):
            @pl.when(z != o)
            def _():
                line_copy(u, o, o, right).wait_send()

    @pl.loop(0, chunks)
    def _(c):
        @pl.when(z < last)
        def _():
            first_gather(c, 0, right).wait_send()

        @pl.when(z > 0)
        def _():
            first_gather(c, 1, left).wait_send()

        for o in range(chips):
            @pl.when(z != o)
            def _():
                twin_copy(c, o).wait_send()

            @pl.when(jnp.logical_and(z > o, z < last))
            def _():
                gather_copy(c, o, right).wait_send()

            @pl.when(jnp.logical_and(z < o, z > 0))
            def _():
                gather_copy(c, o, left).wait_send()


def exchange(distance, count, inputs, cotangent, tokens, weight, master, first, second):
    groups, members = lax.axis_size("dp"), lax.axis_size("fsdp")
    rows, columns = weight.shape
    window = inputs.shape[0]
    chips, chunks = members // 2, columns // WIDTH
    whole = pl.BlockSpec(memory_space=pl.ANY)
    dma = pltpu.SemaphoreType.DMA
    units = chunks * SPLIT
    block = (rows, WIDTH)
    half = (rows // SPLIT, WIDTH)
    return pl.pallas_call(
        partial(kernel, chips, groups, chunks, distance),
        out_shape=(
            jax.ShapeDtypeStruct((chips, 2, rows, columns), weight.dtype),
            jax.ShapeDtypeStruct((tokens.shape[0], columns), jnp.bfloat16),
            jax.ShapeDtypeStruct((3, rows, columns), jnp.bfloat16),
            jax.ShapeDtypeStruct((3, rows, columns), jnp.bfloat16),
        ),
        in_specs=[pl.BlockSpec(memory_space=pltpu.SMEM)] + [whole] * 7,
        out_specs=(whole,) * 4,
        scratch_shapes=[
            pltpu.VMEM((2, window, rows), jnp.bfloat16),
            pltpu.VMEM((chips, rows, window), jnp.bfloat16),
            pltpu.VMEM((2, chips, rows, window), jnp.bfloat16),
            pltpu.VMEM((2, window, columns), jnp.bfloat16),
            pltpu.VMEM((members, 8, 128), jnp.float32),
            pltpu.VMEM((chunks, chips) + block, jnp.bfloat16),
            pltpu.VMEM((chunks, chips + 1) + block, jnp.bfloat16),
            pltpu.VMEM((2, 3) + half, jnp.float32),
            pltpu.VMEM((STAGES, 3) + half, jnp.bfloat16),
            pltpu.VMEM(tokens.shape, jnp.bfloat16),
            pltpu.VMEM((tokens.shape[0], 2 * WIDTH), jnp.float32),
            pltpu.VMEM((2, tokens.shape[0], 2 * WIDTH), jnp.bfloat16),
            dma((members,)), dma((members,)),
            dma((2,)), dma((chips,)), dma((chips,)), dma(()), dma(()), dma(()),
            dma((units, chips)), dma((units, chips + 1)),
            dma((chunks, chips + 1)), dma((chunks, chips)),
            dma(()), dma(()),
            dma((chunks, chips)), dma((chunks, chips)),
            dma((units,)), dma((units,)),
            dma((2, 3)), dma((STAGES,)),
            dma(()), dma((chips, 2)), dma((2,)),
        ],
        compiler_params=pltpu.CompilerParams(
            collective_id=distance, has_side_effects=True, vmem_limit_bytes=63 * 1024 * 1024
        ),
        name=f"exchange_{distance}",
    )(count, inputs, cotangent, tokens, weight, master, first, second)


def finish_kernel(forward, kept, copies, *outs):
    outs[0][...] = forward[...]
    for i in range(3):
        outs[1 + i][...] = kept[i].astype(jnp.float32)
        outs[4 + i][...] = copies[i].astype(jnp.float32)


def finish(forward, kept, copies):
    count, columns = forward.shape
    rows = kept.shape[1]
    steps = rows // BAND
    tile = pl.BlockSpec((BAND, columns), lambda j: (j, 0))
    three = pl.BlockSpec((3, BAND, columns), lambda j: (0, j, 0))
    front = pl.BlockSpec((count // steps, columns), lambda j: (j, 0))
    return pl.pallas_call(
        finish_kernel,
        grid=(steps,),
        in_specs=[front, three, three],
        out_specs=[front] + [tile] * 6,
        out_shape=[jax.ShapeDtypeStruct((count, columns), jnp.bfloat16)]
        + [jax.ShapeDtypeStruct((rows, columns), jnp.float32)] * 6,
        compiler_params=pltpu.CompilerParams(vmem_limit_bytes=56 * 1024 * 1024),
        name="finish",
    )(forward, kept, copies)


def body(
    activations,
    cotangent,
    next_input,
    next_weight,
    master,
    first_moment,
    second_moment,
    token_counts,
    peer_groups,
):
    groups = lax.axis_size("dp")
    branches = [partial(exchange, distance) for distance in range(1, groups)]
    gathered, forward, kept, copies = lax.switch(
        jnp.clip(peer_groups[0] - 1, 0, groups - 2), branches,
        token_counts, activations, cotangent, next_input, next_weight, master, first_moment, second_moment,
    )
    return tuple(finish(forward, kept, copies))


def solution(mesh):
    return jax.shard_map(
        body,
        mesh=mesh,
        in_specs=(
            P("fsdp", None),
            P("fsdp", "dp"),
            P("fsdp", None),
            P("fsdp", "dp"),
            P("fsdp", "dp"),
            P("fsdp", "dp"),
            P("fsdp", "dp"),
            P("fsdp"),
            P(),
        ),
        out_specs=(P("fsdp", "dp"),) * 7,
        check_vma=False,
    )
```

```python
from functools import partial

import jax
import jax.numpy as jnp
from jax import lax
from jax.experimental import pallas as pl
from jax.experimental.pallas import tpu as pltpu
from jax.sharding import PartitionSpec as P

beta_first = 0.9
beta_second = 0.95
epsilon = 1e-05
learn_rate = 0.00015
decay_rate = 0.1

MESH = pl.DeviceIdType.MESH
WIDTH = 128
HOP = 1
RELAY = 1
AHEAD = 0
LEAD = 6
SPLIT = 1
PARTS = 8
STAGES = 8
BAND = 64


def adam_update(master, first_moment, second_moment, gradient):
    new_first = beta_first * first_moment + (1.0 - beta_first) * gradient
    new_second = beta_second * second_moment + (1.0 - beta_second) * gradient * gradient
    new_master = master - learn_rate * (
        new_first / (jnp.sqrt(new_second) + epsilon) + decay_rate * master
    )
    return (new_master, new_first, new_second)


def kernel(
    chips, groups, chunks, distance,
    count, inputs, cotangent, tokens, weight, master, first, second,
    gathered, forward, kept, copies,
    loaded, outgoing, turned, rights, counts, paired, arrived, state, staged,
    held, summed, result,
    count_send, count_recv, load_sem, turn_send, turn_recv, right_send, right_recv, right_sem,
    line_send, line_recv, gather_send, gather_recv, whole_send, whole_recv,
    twin_send, twin_recv, copy_send, copy_recv, state_sem, own_sem, held_sem, wide_sem, result_sem,
):
    g = lax.axis_index("dp")
    f = lax.axis_index("fsdp")
    z = f // 2
    core = f % 2
    members = 2 * chips
    rows = weight.shape[0]
    strip = rows // SPLIT
    piece = strip // PARTS
    units = chunks * SPLIT
    batch = 2 * SPLIT
    last = chips - 1
    finish = HOP * last
    twin = (g, z * 2 + 1 - core)
    right = (g, ((z + 1) % chips) * 2 + core)
    left = (g, ((z + chips - 1) % chips) * 2 + core)
    peer = ((g + distance) % groups, f)
    giver = ((g + groups - distance) % groups, f)

    def span(u):
        return pl.ds(pl.multiple_of((u % SPLIT) * strip, strip), strip)

    def cols(c):
        return pl.ds(pl.multiple_of(c * WIDTH, WIDTH), WIDTH)

    def area(u):
        c = u // SPLIT
        return span(u), pl.ds(pl.multiple_of(c * WIDTH, WIDTH), WIDTH)

    def remote(src, dst, send, recv, device):
        return pltpu.make_async_remote_copy(
            src_ref=src, dst_ref=dst, send_sem=send, recv_sem=recv,
            device_id=device, device_id_type=MESH,
        )

    def count_copy(k, slot, device):
        part = counts.at[slot]
        return remote(part, part, count_send.at[k], count_recv.at[k], device)

    def input_load(d, plane, slot):
        start = pl.multiple_of((2 * d + plane) * rows, rows)
        return pltpu.make_async_copy(inputs.at[:, pl.ds(start, rows)], loaded.at[slot], load_sem.at[slot])

    def turn_copy(d):
        return remote(outgoing.at[d], turned.at[1, d], turn_send.at[d], turn_recv.at[d], twin)

    def line_copy(c, d, slot, device):
        return remote(paired.at[c // SPLIT, d, span(c)], arrived.at[c // SPLIT, slot, span(c)],
                      line_send.at[c, d], line_recv.at[c, slot], device)

    def first_gather(c, way, device):
        return remote(weight.at[:, cols(c)], gathered.at[z, core, :, cols(c)],
                      gather_send.at[c, chips if way else z], gather_recv.at[c, z], device)

    def gather_copy(c, o, device):
        part = gathered.at[o, core, :, cols(c)]
        return remote(part, part, gather_send.at[c, o], gather_recv.at[c, o], device)

    def twin_copy(c, o):
        part = gathered.at[o, core, :, cols(c)]
        return remote(part, part, twin_send.at[c, o], twin_recv.at[c, o], twin)

    def twin_arrival(c, o):
        part = gathered.at[o, 1 - core, :, cols(c)]
        return remote(part, part, twin_send.at[c, o], twin_recv.at[c, o], twin)

    def peer_copy(c):
        return remote(staged.at[c % STAGES], copies.at[(slice(None),) + area(c)], copy_send.at[c], copy_recv.at[c], peer)

    def state_loads(c):
        return [
            pltpu.make_async_copy(ref.at[area(c)], state.at[c % 2, i], state_sem.at[c % 2, i])
            for i, ref in enumerate((master, first, second))
        ]

    def own_store(c):
        return pltpu.make_async_copy(
            staged.at[c % STAGES], kept.at[(slice(None),) + area(c)], own_sem.at[c % STAGES]
        )

    def wide(j):
        return pl.ds(pl.multiple_of(j * (2 * WIDTH), 2 * WIDTH), 2 * WIDTH)

    def wide_load(j, o, q, source):
        return pltpu.make_async_copy(
            source, outgoing.at[o, :, pl.ds(q * 2 * WIDTH, 2 * WIDTH)], wide_sem.at[o, q],
        )

    def start_wide(j):
        for o in range(chips):
            wide_load(j, o, 1, gathered.at[o, 1 - core, :, wide(j)]).start()

            @pl.when(z == o)
            def _():
                wide_load(j, o, 0, weight.at[:, wide(j)]).start()

            @pl.when(z != o)
            def _():
                wide_load(j, o, 0, gathered.at[o, core, :, wide(j)]).start()

    def wait_wide(j):
        for o in range(chips):
            for q in range(2):
                wide_load(j, o, q, weight.at[:, wide(j)]).wait()

    def result_store(j):
        return pltpu.make_async_copy(result.at[j % 2], forward.at[:, wide(j)], result_sem.at[j % 2])

    def add_into(u, d):
        c, base = u // SPLIT, (u % SPLIT) * strip

        @pl.loop(0, PARTS)
        def _(i):
            part = pl.ds(pl.multiple_of(base + i * piece, piece), piece)
            total_part = paired[c, d, part, :].astype(jnp.float32) + arrived[c, d, part, :].astype(jnp.float32)
            paired[c, d, part, :] = total_part.astype(jnp.bfloat16)

    def within(u):
        return jnp.logical_and(u >= 0, u < units)

    def inside(c):
        return jnp.logical_and(c >= 0, c < chunks)

    def issued(t, position):
        total = LEAD + (t + 1)
        for k in range(1, chips):
            total = total + jnp.where(
                position + k <= last, jnp.minimum(t + 1, HOP * (last - k) // SPLIT), 0
            )
            total = total + jnp.where(k <= position, jnp.minimum(t + 1, RELAY * k), 0)
        return jnp.minimum(total, chunks)

    def send_own(low_right, high_right, low_left, high_left):
        @pl.when(z < last)
        def _():
            @pl.loop(low_right, high_right)
            def _(c):
                first_gather(c, 0, right).start()

        @pl.when(z > 0)
        def _():
            @pl.loop(low_left, high_left)
            def _(c):
                first_gather(c, 1, left).start()

    barrier = pltpu.get_barrier_semaphore()
    others = [(g, (f + k) % members) for k in range(1, members)]
    greeted = others + [peer, giver]
    for device in greeted:
        pl.semaphore_signal(barrier, inc=1, device_id=device, device_id_type=MESH)
    pl.semaphore_wait(barrier, len(greeted))

    send_own(0, issued(AHEAD - 1, z), 0, issued(AHEAD - 1, last - z))
    right_copy = remote(cotangent, rights.at[1], right_send, right_recv, twin)
    right_copy.start()
    right_load = pltpu.make_async_copy(cotangent, rights.at[0], right_sem)
    right_load.start()
    order = [(d, 1) for d in range(chips)] + [(d, 0) for d in range(chips)]

    def turn_load(k):
        d, mine = order[k]
        return input_load(d, 1 - core if mine else core, k % 2)

    turn_load(0).start()
    held_load = pltpu.make_async_copy(tokens, held, held_sem)
    held_load.start()
    counts[f] = jnp.full(counts.shape[1:], count[0].astype(jnp.float32))
    for k, device in enumerate(others):
        count_copy(k, f, device).start()

    for k in range(2 * chips):
        if k + 1 < 2 * chips:
            turn_load(k + 1).start()
        turn_load(k).wait()
        d, mine = order[k]
        block = loaded[k % 2]
        live = lax.broadcasted_iota(jnp.int32, block.shape, 0) < count[0]
        block = jnp.where(live, block, jnp.zeros((), block.dtype)).T
        if mine:
            outgoing[d] = block
            turn_copy(d).start()
        else:
            turned[0, d] = block

    whole_copy = remote(weight, gathered.at[z, core], whole_send, whole_recv, twin)
    whole_copy.start()

    def multiply(j):
        @pl.loop(0, chips)
        def _(d):
            product = jnp.dot(turned[0, d], rights[0, :, wide(j)], preferred_element_type=jnp.float32)
            product += jnp.dot(turned[1, d], rights[1, :, wide(j)], preferred_element_type=jnp.float32)
            product = product.astype(jnp.bfloat16)
            paired[2 * j, d] = product[:, :WIDTH]
            paired[2 * j + 1, d] = product[:, WIDTH:]

    def project(j):
        wait_wide(j)

        def part(o):
            total = None
            for q, plane in enumerate((core, 1 - core)):
                start = pl.multiple_of((2 * o + plane) * rows, rows)
                product = jnp.dot(
                    held[:, pl.ds(start, rows)], outgoing[o, :, q * 2 * WIDTH:(q + 1) * 2 * WIDTH],
                    preferred_element_type=jnp.float32,
                )
                total = product if q == 0 else total + product
            return total

        summed[...] = part(0)

        @pl.loop(1, chips)
        def _(o):
            summed[...] += part(o)

        @pl.when(j >= 2)
        def _():
            result_store(j - 2).wait()

        result[j % 2] = summed[...].astype(jnp.bfloat16)
        result_store(j).start()

    right_load.wait()
    right_copy.wait_recv()
    for d in range(chips):
        turn_copy(d).wait_recv()
    multiply(0)
    for k in range(members - 1):
        count_copy(k, (f + members - 1 - k) % members, others[k]).wait_recv()

    def update(u, slots):
        c, base, slot = u // SPLIT, (u % SPLIT) * strip, u % 2
        share = 1.0 / jnp.sum(counts[:, :1, :], axis=0)

        @pl.loop(0, PARTS)
        def _(i):
            here = pl.ds(pl.multiple_of(base + i * piece, piece), piece)
            part = pl.ds(pl.multiple_of(i * piece, piece), piece)
            gradient = paired[c, z, here, :].astype(jnp.float32)
            for k in slots:
                gradient += arrived[c, k, here, :].astype(jnp.float32)
            results = adam_update(
                state[slot, 0, part, :], state[slot, 1, part, :], state[slot, 2, part, :], gradient * share
            )
            for k, value in enumerate(results):
                staged[u % STAGES, k, part, :] = value.astype(jnp.bfloat16)

    @pl.loop(0, units + max(finish, SPLIT * (RELAY * last + 2 - AHEAD)))
    def _(t):
        coming = t + 1 - finish

        @pl.when(within(coming))
        def _():
            for copy in state_loads(coming):
                copy.start()

        for d in range(chips):
            e = last - d
            rightward = t - HOP * (z + last - e)

            @pl.when(jnp.logical_and(z < e, within(rightward)))
            def _():
                @pl.when(z > 0)
                def _():
                    line_copy(rightward, e, e, left).wait_recv()
                    add_into(rightward, e)

                line_copy(rightward, e, e, right).start()

            leftward = t - HOP * (last - z + d)

            @pl.when(jnp.logical_and(z > d, within(leftward)))
            def _():
                @pl.when(z < last)
                def _():
                    line_copy(leftward, d, d, right).wait_recv()
                    add_into(leftward, d)

                @pl.when(z == d + 1)
                def _():
                    line_copy(leftward, d, chips, left).start()

                @pl.when(z > d + 1)
                def _():
                    line_copy(leftward, d, d, left).start()

        done = t - finish

        @pl.when(within(done))
        def _():
            for copy in state_loads(done):
                copy.wait()

            @pl.when(done >= STAGES)
            def _():
                peer_copy(done - STAGES).wait_send()
                own_store(done - STAGES).wait()

            @pl.when(z > 0)
            def _():
                for d in range(1, chips):
                    @pl.when(z == d)
                    def _():
                        line_copy(done, d, d, left).wait_recv()

            @pl.when(z < last)
            def _():
                line_copy(done, 0, chips, right).wait_recv()

            @pl.when(z == 0)
            def _():
                update(done, [chips])

            @pl.when(z == last)
            def _():
                update(done, [last])

            @pl.when(jnp.logical_and(z > 0, z < last))
            def _():
                update(done, [z, chips])

            peer_copy(done).start()
            own_store(done).start()

        q = t // SPLIT + AHEAD

        @pl.when(t % SPLIT == 0)
        def _():
            send_own(issued(q - 1, z), issued(q, z), issued(q - 1, last - z), issued(q, last - z))

            for o in range(chips):
                from_left = q - RELAY * (z - o)
                from_right = q - RELAY * (o - z)

                @pl.when(jnp.logical_and(z > o, inside(from_left)))
                def _():
                    gather_copy(from_left, o, left).wait_recv()

                    @pl.when(z < last)
                    def _():
                        gather_copy(from_left, o, right).start()

                    twin_copy(from_left, o).start()

                @pl.when(jnp.logical_and(z < o, inside(from_right)))
                def _():
                    gather_copy(from_right, o, right).wait_recv()

                    @pl.when(z > 0)
                    def _():
                        gather_copy(from_right, o, left).start()

                    twin_copy(from_right, o).start()

        ready = q - RELAY * last - 1

        @pl.when(jnp.logical_and(ready == 0, t % SPLIT == 0))
        def _():
            held_load.wait()
            whole_copy.wait_recv()
            for d in range(chips):
                turn_copy(d).wait_send()

        @pl.when(jnp.logical_and(inside(ready), t % SPLIT == 0))
        def _():
            for o in range(chips):
                @pl.when(z != o)
                def _():
                    twin_arrival(ready, o).wait_recv()

            @pl.when(ready % 2 == 1)
            def _():
                start_wide(ready // 2)

        @pl.when(jnp.logical_and(inside(ready), jnp.logical_and(ready % 2 == 1, t % SPLIT == SPLIT - 1)))
        def _():
            project(ready // 2)

        @pl.when(jnp.logical_and(t % batch == batch - 1, t + 1 < units))
        def _():
            multiply((t + 1) // batch)

    right_copy.wait_send()
    whole_copy.wait_send()
    for j in range(max(chunks // 2 - 2, 0), chunks // 2):
        result_store(j).wait()
    for k in range(members - 1):
        count_copy(k, f, others[k]).wait_send()
    for c in range(max(units - STAGES, 0), units):
        peer_copy(c).wait_send()
        own_store(c).wait()

    @pl.loop(0, units)
    def _(u):
        peer_copy(u).wait_recv()
        for o in range(chips):
            @pl.when(z != o)
            def _():
                line_copy(u, o, o, right).wait_send()

    @pl.loop(0, chunks)
    def _(c):
        @pl.when(z < last)
        def _():
            first_gather(c, 0, right).wait_send()

        @pl.when(z > 0)
        def _():
            first_gather(c, 1, left).wait_send()

        for o in range(chips):
            @pl.when(z != o)
            def _():
                twin_copy(c, o).wait_send()

            @pl.when(jnp.logical_and(z > o, z < last))
            def _():
                gather_copy(c, o, right).wait_send()

            @pl.when(jnp.logical_and(z < o, z > 0))
            def _():
                gather_copy(c, o, left).wait_send()


def exchange(distance, count, inputs, cotangent, tokens, weight, master, first, second):
    groups, members = lax.axis_size("dp"), lax.axis_size("fsdp")
    rows, columns = weight.shape
    window = inputs.shape[0]
    chips, chunks = members // 2, columns // WIDTH
    whole = pl.BlockSpec(memory_space=pl.ANY)
    dma = pltpu.SemaphoreType.DMA
    units = chunks * SPLIT
    block = (rows, WIDTH)
    half = (rows // SPLIT, WIDTH)
    return pl.pallas_call(
        partial(kernel, chips, groups, chunks, distance),
        out_shape=(
            jax.ShapeDtypeStruct((chips, 2, rows, columns), weight.dtype),
            jax.ShapeDtypeStruct((tokens.shape[0], columns), jnp.bfloat16),
            jax.ShapeDtypeStruct((3, rows, columns), jnp.bfloat16),
            jax.ShapeDtypeStruct((3, rows, columns), jnp.bfloat16),
        ),
        in_specs=[pl.BlockSpec(memory_space=pltpu.SMEM)] + [whole] * 7,
        out_specs=(whole,) * 4,
        scratch_shapes=[
            pltpu.VMEM((2, window, rows), jnp.bfloat16),
            pltpu.VMEM((chips, rows, window), jnp.bfloat16),
            pltpu.VMEM((2, chips, rows, window), jnp.bfloat16),
            pltpu.VMEM((2, window, columns), jnp.bfloat16),
            pltpu.VMEM((members, 8, 128), jnp.float32),
            pltpu.VMEM((chunks, chips) + block, jnp.bfloat16),
            pltpu.VMEM((chunks, chips + 1) + block, jnp.bfloat16),
            pltpu.VMEM((2, 3) + half, jnp.float32),
            pltpu.VMEM((STAGES, 3) + half, jnp.bfloat16),
            pltpu.VMEM(tokens.shape, jnp.bfloat16),
            pltpu.VMEM((tokens.shape[0], 2 * WIDTH), jnp.float32),
            pltpu.VMEM((2, tokens.shape[0], 2 * WIDTH), jnp.bfloat16),
            dma((members,)), dma((members,)),
            dma((2,)), dma((chips,)), dma((chips,)), dma(()), dma(()), dma(()),
            dma((units, chips)), dma((units, chips + 1)),
            dma((chunks, chips + 1)), dma((chunks, chips)),
            dma(()), dma(()),
            dma((chunks, chips)), dma((chunks, chips)),
            dma((units,)), dma((units,)),
            dma((2, 3)), dma((STAGES,)),
            dma(()), dma((chips, 2)), dma((2,)),
        ],
        compiler_params=pltpu.CompilerParams(
            collective_id=distance, has_side_effects=True, vmem_limit_bytes=63 * 1024 * 1024
        ),
        name=f"exchange_{distance}",
    )(count, inputs, cotangent, tokens, weight, master, first, second)


def finish_kernel(forward, kept, copies, *outs):
    outs[0][...] = forward[...]
    for i in range(3):
        outs[1 + i][...] = kept[i].astype(jnp.float32)
        outs[4 + i][...] = copies[i].astype(jnp.float32)


def finish(forward, kept, copies):
    count, columns = forward.shape
    rows = kept.shape[1]
    steps = rows // BAND
    tile = pl.BlockSpec((BAND, columns), lambda j: (j, 0))
    three = pl.BlockSpec((3, BAND, columns), lambda j: (0, j, 0))
    front = pl.BlockSpec((count // steps, columns), lambda j: (j, 0))
    return pl.pallas_call(
        finish_kernel,
        grid=(steps,),
        in_specs=[front, three, three],
        out_specs=[front] + [tile] * 6,
        out_shape=[jax.ShapeDtypeStruct((count, columns), jnp.bfloat16)]
        + [jax.ShapeDtypeStruct((rows, columns), jnp.float32)] * 6,
        compiler_params=pltpu.CompilerParams(vmem_limit_bytes=56 * 1024 * 1024),
        name="finish",
    )(forward, kept, copies)


def body(
    activations,
    cotangent,
    next_input,
    next_weight,
    master,
    first_moment,
    second_moment,
    token_counts,
    peer_groups,
):
    groups = lax.axis_size("dp")
    branches = [partial(exchange, distance) for distance in range(1, groups)]
    gathered, forward, kept, copies = lax.switch(
        jnp.clip(peer_groups[0] - 1, 0, groups - 2), branches,
        token_counts, activations, cotangent, next_input, next_weight, master, first_moment, second_moment,
    )
    return tuple(finish(forward, kept, copies))


def solution(mesh):
    return jax.shard_map(
        body,
        mesh=mesh,
        in_specs=(
            P("fsdp", None),
            P("fsdp", "dp"),
            P("fsdp", None),
            P("fsdp", "dp"),
            P("fsdp", "dp"),
            P("fsdp", "dp"),
            P("fsdp", "dp"),
            P("fsdp"),
            P(),
        ),
        out_specs=(P("fsdp", "dp"),) * 7,
        check_vma=False,
    )
```
